32 devices in a mesh: wide: 4 (over x, core), narrow: 8 (over z, y).
Axes of the slice: x: 2, y: 2, z: 4, core: 2. Of those that a mesh axis runs over, the one named last changes fastest.
Arguments:
- grad_parts: bfloat16 [4, 3584, 8192], P('wide', 'narrow'), may hold values from -6 to 6
- master: bfloat16 [3584, 8192], P('narrow'), may hold values from -0.1875 to 0.1875
- moment_one: float32 [3584, 8192], P('narrow'), may hold values from -4 to 4
- moment_two: float32 [3584, 8192], P('narrow'), may hold values from 0.01 to 1
- gate_up: bfloat16 [3584, 2, 8192], P(None, None, 'narrow'), may hold values from -0.09375 to 0.09375
- tokens: bfloat16 [64, 3584], P(('wide', 'narrow')), may hold values from -6 to 6
- expert_ids: int32 [64, 4], P(('wide', 'narrow')), may hold values from 0 to 7, all different within a row; in each aligned block of 2 rows (0 to 1, 2 to 3, ...) at most 2 rows name the same one
- gate_vals: bfloat16 [64, 4], P(('wide', 'narrow')), may hold values from 0.049804688 to 1
Outputs:
- new_master: bfloat16 [3584, 8192], P('narrow')
- new_one: float32 [3584, 8192], P('narrow')
- new_two: float32 [3584, 8192], P('narrow')
- combined: bfloat16 [64, 3584], P(('wide', 'narrow'))
The draws below stay inside these ranges and needn't reach their ends.
Inputs may be any that keep to these rules, and one draw needn't show every extreme that they name: `expert_ids`: each token names 4 distinct experts; each device's 2 tokens name every expert at most 2 times (which follows from the distinct ids), and some device names one expert twice.
All inputs are finite; a program needn't handle non-finite values.
Results may differ from the reference program's by a relative error of at most 0.022.
Values may be sent and summed in bfloat16 or wider, within the bound.
No kernel may reach another device: no remote copies, remote signals or barrier semaphores. Data moves between devices by JAX's collectives and lax.ppermute only.
A program may use at most 192 MiB of HBM per device.

```python
import math
import jax
import jax.numpy as jnp
import numpy as np
from jax import lax

D = 3584
FF = 1024
EXPERTS = 8
TOPK = 4
QBLOCK = 128
TOK_DEV = 2
CAP = 2
TOKENS = 64
N_WIDE = 4
N_NARROW = 8


def steps_of(own_key, shape, shards, smallest, top_value):
    def one(position, shards_of):
        heights = jax.random.uniform(jax.random.fold_in(jax.random.fold_in(own_key, 6), position), (shards_of,), jnp.float32, smallest / len(shards), top_value / len(shards))
        return jnp.repeat(jnp.exp(heights), shape[position] // shards_of).reshape((-1,) + (1,) * (len(shape) - position - 1))

    gain = one(*shards[0])
    for cut in shards[1:]:
        gain = gain * one(*cut)
    return gain


def assign_block(own_key, own, number, rows, count, top, reach, slope):
    sequence = jax.random.permutation(own_key, count)
    heavy_load, common = shares(count, rows * top, reach, slope, True), shares(count, rows * top, reach, slope, False)
    places = jnp.arange(count)

    def named(sizes, turn):
        used = int((sizes > 0).sum())
        fixed = max(1, used // 4)
        moved = fixed + (places - fixed + turn * (used - fixed)) % max(1, count - fixed)
        return jnp.zeros((count,), jnp.int32).at[sequence[jnp.where(places < fixed, places, moved)]].set(jnp.asarray(sizes, jnp.int32))

    sizes = jnp.where(number % 4 == 0, named(heavy_load, number // 4), named(common, number - number // 4 - 1))
    mixed = jax.random.permutation(jax.random.fold_in(own, 3), count)
    source_of, receiver = mixed[0:count // 2 * 2:2], mixed[1:count // 2 * 2:2]
    slack = jnp.minimum(sizes[source_of] - 1, reach - sizes[receiver]) // 2
    slack = jnp.where((source_of == sequence[0]) | (receiver == sequence[0]) | (sizes[receiver] == 0), 0, jnp.maximum(slack, 0))
    moved = jax.random.randint(jax.random.fold_in(own, 4), (count // 2,), 0, 1 << 20) % (slack + 1)
    sizes = sizes.at[source_of].add(-moved).at[receiver].add(moved)
    members = jnp.searchsorted(jnp.cumsum(sizes), jnp.arange(rows * top), side="right").astype(jnp.int32)
    listing = members.reshape(top, rows).T
    listing = listing[jax.random.permutation(jax.random.fold_in(own, 1), rows)]
    turn = jax.random.randint(jax.random.fold_in(own, 2), (rows, 1), 0, top)
    return jnp.take_along_axis(listing, (jnp.arange(top)[None, :] + turn) % top, axis=1)


def shares(count, total, limit, lean, full):
    loads = [(1 << 20) // math.isqrt(grade ** lean) + 1 for grade in range(1, count + 1)]
    largest = limit if full else min(limit, max(-(-total // count), total * loads[0] // sum(loads)))
    least = 1 if total - largest >= count - 1 else 0
    counts, surplus = [largest] + [least] * (count - 1), total - largest - least * (count - 1)
    while surplus > 0:
        free = [i for i in range(1, count) if counts[i] < largest] or [i for i in range(1, count) if counts[i] < limit]
        pool, remaining = sum([loads[i] for i in free]), surplus
        for i in free:
            addition = min(limit - counts[i], max(1, remaining * loads[i] // pool), surplus)
            counts[i] = counts[i] + addition
            surplus = surplus - addition
    return np.array(counts)


def gaussian(rng, extent, deviation, reach, split=(), held_as=jnp.bfloat16):
    entries = jax.random.normal(rng, extent, jnp.float32) * deviation
    if len(split) > 0:
        entries = steps_of(rng, extent, split, -0.22, 0.18) * entries
    return jnp.clip(entries, min=-reach, max=reach).astype(held_as)


def setup_inputs(seed: int = 0) -> dict:
    splits = jax.random.split(jax.random.key(seed), 9)
    grad_parts = gaussian(splits[0], (N_WIDE, D, EXPERTS * FF), 1.0, 6.0, ((0, 4), (1, 8)))
    master = gaussian(splits[1], (D, EXPERTS * FF), FF ** -0.5, 0.1875, ((0, 8),))
    moment_one = gaussian(splits[2], (D, EXPERTS * FF), 0.3, 4.0, ((0, 8),), jnp.float32)
    moment_two = jnp.clip(jnp.exp(math.log(1.0) - 4.6051702 * jax.random.uniform(splits[3], (D, EXPERTS * FF), jnp.float32) ** steps_of(splits[3], (D, EXPERTS * FF), ((0, 8),), -0.2, 0.2)), 0.01, 1.0)
    gate_up = gaussian(splits[4], (D, 2, EXPERTS * FF), D ** -0.5, 0.09375, ((2, 8),))
    tokens = gaussian(splits[5], (TOKENS, D), 1.0, 6.0, ((0, 32),))
    expert_ids_keys = jax.random.split(jax.random.fold_in(splits[6], 1), TOKENS // TOK_DEV)
    expert_ids_turns = jax.random.permutation(jax.random.fold_in(splits[6], 3), TOKENS // TOK_DEV)
    expert_ids = jax.vmap(lambda own, number: assign_block(jax.random.fold_in(splits[6], 2), own, number, TOK_DEV, EXPERTS, TOPK, CAP, 2))(expert_ids_keys, expert_ids_turns).reshape((TOKENS, TOPK))
    gate_vals = jnp.clip(0.049804688 + 0.9501953 * jax.random.uniform(splits[7], (TOKENS, TOPK), jnp.float32) ** steps_of(splits[7], (TOKENS, TOPK), ((0, 32),), -0.2, 0.2), 0.049804688, 1.0).astype(jnp.bfloat16)
    return {"grad_parts": grad_parts, "master": master, "moment_one": moment_one, "moment_two": moment_two, "gate_up": gate_up, "tokens": tokens, "expert_ids": expert_ids, "gate_vals": gate_vals}


beta_first = 0.9
beta_second = 0.95
learn_rate = 0.003
adam_eps = 1e-08
quant_limit = 448.0
amax_eps = 1e-06
bias_first = 1.0 - 0.9 ** 10
bias_second = 1.0 - 0.95 ** 10

def adam_quant(grad_sum, master, moment_one, moment_two):
    new_one = beta_first * moment_one + (1.0 - beta_first) * grad_sum
    new_two = beta_second * moment_two + (1.0 - beta_second) * grad_sum * grad_sum
    step_dir = new_one / bias_first / (jnp.sqrt(new_two / bias_second) + adam_eps)
    updated = master.astype(jnp.float32) - learn_rate * step_dir
    row_count, col_count = updated.shape
    blocks = updated.reshape(row_count, col_count // QBLOCK, QBLOCK)
    scales = ((lax.optimization_barrier(jnp.max(jnp.abs(blocks), axis=2)) + amax_eps) / quant_limit).astype(jnp.bfloat16)
    quanta = (blocks / scales.astype(jnp.float32)[:, :, None]).astype(jnp.bfloat16).reshape(row_count, col_count)
    return (updated.astype(jnp.bfloat16), new_one, new_two, quanta, scales)

def expert_rows(rows_in, gate_piece, quanta, scales):
    unit_count = gate_piece.shape[2]
    proj_both = jnp.dot(rows_in, gate_piece.reshape(gate_piece.shape[0], 2 * unit_count), preferred_element_type=jnp.float32)
    hidden = (jax.nn.silu(proj_both[:, :unit_count]) * proj_both[:, unit_count:]).astype(jnp.bfloat16)
    block_count = unit_count // QBLOCK
    per_block = jnp.einsum('rbf,dbf->rbd', hidden.reshape(-1, block_count, QBLOCK).astype(jnp.float32), quanta.reshape(quanta.shape[0], block_count, QBLOCK).astype(jnp.float32))
    return jnp.einsum('rbd,db->rd', per_block, scales.astype(jnp.float32))

def reference(grad_parts, master, moment_one, moment_two, gate_up, tokens, expert_ids, gate_vals):
    grad_sum = jnp.zeros(master.shape, jnp.float32)
    for replica in range(N_WIDE):
        grad_sum = grad_sum + grad_parts[replica].astype(jnp.float32)
    new_master, new_one, new_two, quanta, scales = adam_quant(grad_sum, master, moment_one, moment_two)
    onehot = (expert_ids[:, :, None] == jnp.arange(EXPERTS, dtype=jnp.int32)[None, None, :]).astype(jnp.float32)
    weights_tok = lax.optimization_barrier(jnp.sum(onehot * gate_vals.astype(jnp.float32)[:, :, None], axis=1))
    unit_count = EXPERTS * FF // N_NARROW
    group_size = N_NARROW // EXPERTS
    block_count = unit_count // QBLOCK

    def add_slice(total, owner):
        piece_gu = lax.dynamic_slice_in_dim(gate_up, owner * unit_count, unit_count, 2)
        piece_q = lax.dynamic_slice_in_dim(quanta, owner * unit_count, unit_count, 1)
        piece_s = lax.dynamic_slice_in_dim(scales, owner * block_count, block_count, 1)
        partial_value = expert_rows(tokens, piece_gu, piece_q, piece_s).astype(jnp.bfloat16).astype(jnp.float32)
        column = owner // group_size
        chosen = (jnp.arange(EXPERTS, dtype=jnp.int32) == column).astype(jnp.float32)
        tok_weight = lax.optimization_barrier(jnp.sum(weights_tok * chosen[None, :], axis=1))
        return (total + tok_weight[:, None] * partial_value, None)
    start_total = jnp.zeros((tokens.shape[0], D), jnp.float32)
    combined = lax.scan(add_slice, start_total, jnp.arange(N_NARROW, dtype=jnp.int32))[0]
    return (new_master, new_one, new_two, combined.astype(jnp.bfloat16))
```

```python
import functools

import jax
import jax.numpy as jnp
from jax import lax
from jax.experimental import pallas as pl
from jax.experimental.pallas import tpu as pltpu
from jax.sharding import PartitionSpec as P

EXPERTS = 8
QBLOCK = 128
LANES = 128

beta_first = 0.9
beta_second = 0.95
learn_rate = 0.003
adam_eps = 1e-08
quant_limit = 448.0
amax_eps = 1e-06
bias_first = 1.0 - 0.9**10
bias_second = 1.0 - 0.95**10


def adam_kernel(pair, aliased, slices, base, *refs):
    refs = list(refs)
    parts = [refs.pop(0) for _ in range(3 if pair else 1)]
    master, one, two, hidden, weight = refs[:5]
    new_master, new_one, new_two, comb = refs[5 + (3 if aliased else 0) :]
    rows, cols = master.shape
    unit = cols // slices
    toks = hidden.shape[0]

    def one_slice(s, total):
        at = pl.ds(pl.multiple_of(s * unit, LANES), unit)
        grad = parts[0][:, at].astype(jnp.float32)
        if pair:
            here = grad + parts[1][:, at].astype(jnp.float32)
            grad = here.astype(jnp.bfloat16).astype(jnp.float32) + parts[2][:, at].astype(jnp.float32)
        first = beta_first * one[:, at] + (1.0 - beta_first) * grad
        second = beta_second * two[:, at] + (1.0 - beta_second) * grad * grad
        new_one[:, at] = first
        new_two[:, at] = second
        step_dir = first / bias_first / (jnp.sqrt(second / bias_second) + adam_eps)
        updated = master[:, at].astype(jnp.float32) - learn_rate * step_dir
        new_master[:, at] = updated.astype(jnp.bfloat16)
        hid = hidden[:, at]
        partial = jnp.zeros((rows, toks), jnp.float32)
        for b in range(unit // QBLOCK):
            cut = slice(b * QBLOCK, (b + 1) * QBLOCK)
            block = updated[:, cut]
            amax = jnp.max(jnp.abs(block), axis=1, keepdims=True)
            scale = ((amax + amax_eps) / quant_limit).astype(jnp.bfloat16).astype(jnp.float32)
            quanta = (block / scale).astype(jnp.bfloat16)
            dots = lax.dot_general(
                quanta, hid[:, cut], (((1,), (1,)), ((), ())), preferred_element_type=jnp.float32
            )
            partial = partial + scale * dots
        partial = partial.astype(jnp.bfloat16).astype(jnp.float32)
        return total + partial * weight[pl.ds(s, 1), :]

    comb[...] = lax.fori_loop(0, slices, one_slice, jnp.zeros((rows, toks), jnp.float32))


def adam_rows(base, parts, state, hidden, weight, outs, count, block):
    master = state[0]
    full, cols = master.shape
    toks = hidden.shape[0]
    pair = len(parts) == 3
    here = pl.BlockSpec((block, cols), lambda i, at: (at[0] + i, 0))
    own = pl.BlockSpec((block, cols), lambda i, at: (i, 0))
    whole = lambda a: pl.BlockSpec(a.shape, lambda i, at: (0, 0))
    part_specs = [here, here, own] if pair else [here]
    in_specs = part_specs + [here] * 3 + [whole(hidden), whole(weight)]
    args = list(parts) + list(state) + [hidden, weight]
    aliases = {}
    if outs is not None:
        aliases = {1 + len(args) + i: i for i in range(3)}
        in_specs += [pl.BlockSpec(memory_space=pl.ANY)] * 3
        args += list(outs)
    cells = count * cols
    result = pl.pallas_call(
        functools.partial(adam_kernel, pair, outs is not None, weight.shape[0]),
        grid_spec=pltpu.PrefetchScalarGridSpec(
            num_scalar_prefetch=1,
            grid=(count // block,),
            in_specs=in_specs,
            out_specs=[here] * 3 + [pl.BlockSpec((block, toks), lambda i, at: (i, 0))],
        ),
        out_shape=[
            jax.ShapeDtypeStruct((full, cols), jnp.bfloat16),
            jax.ShapeDtypeStruct((full, cols), jnp.float32),
            jax.ShapeDtypeStruct((full, cols), jnp.float32),
            jax.ShapeDtypeStruct((count, toks), jnp.float32),
        ],
        input_output_aliases=aliases,
        cost_estimate=pl.CostEstimate(
            flops=cells * (30 + 2 * toks), bytes_accessed=cells * 26, transcendentals=cells * 3
        ),
    )(base.reshape(1), *args)
    return result[:3], result[3]


def expert_front(tokens, expert_ids, gate_vals, gate_up):
    narrow = lax.axis_size("narrow")
    tok_count, width = tokens.shape
    onehot = (expert_ids[:, :, None] == jnp.arange(EXPERTS, dtype=jnp.int32)).astype(jnp.float32)
    local = jnp.sum(onehot * gate_vals.astype(jnp.float32)[:, :, None], axis=1)
    local = jnp.pad(local, ((0, 0), (0, LANES - EXPERTS))).astype(jnp.bfloat16)
    packed = jnp.concatenate([tokens, local], axis=1)

    def gather(x):
        out = lax.all_to_all(
            jnp.broadcast_to(x[None], (narrow,) + x.shape), "narrow", 0, 0, tiled=True
        )
        return out

    every = gather(packed).reshape(narrow * tok_count, -1)
    rows, chosen = every[:, :width], every[:, width : width + EXPERTS].astype(jnp.float32)
    proj = jnp.einsum("td,dgu->gtu", rows, gate_up, preferred_element_type=jnp.float32)
    hidden = (jax.nn.silu(proj[0]) * proj[1]).astype(jnp.bfloat16)
    spread = gather(hidden)
    hidden = spread.transpose(1, 0, 2).reshape(narrow * tok_count, -1)
    weight = jnp.repeat(chosen.T, narrow // EXPERTS, axis=0)
    return hidden, weight


def give_back(comb, tok_count):
    narrow = lax.axis_size("narrow")
    rows = comb.shape[0]
    out = comb.T.astype(jnp.bfloat16).reshape(narrow, tok_count, rows)
    out = lax.all_to_all(out, "narrow", 0, 0, tiled=True)
    return out.transpose(1, 0, 2).reshape(tok_count, narrow * rows)


def chunks_of(half):
    sizes, left = [], half
    for share in (48, 48, 48, 32, 24, 16, 8):
        take = min(left, max(8, half * share // 224 // 8 * 8))
        if take:
            sizes.append(take)
        left -= take
    sizes[0] += left
    return sizes


def body(grad_parts, master, moment_one, moment_two, gate_up, tokens, expert_ids, gate_vals):
    grads = grad_parts[0]
    full, cols = grads.shape
    wide = lax.axis_size("wide")
    state = (master, moment_one, moment_two)
    zero = jnp.zeros((), jnp.int32)
    if wide != 4 or full % 32:
        total = lax.psum(grads, "wide")
        hidden, weight = expert_front(tokens, expert_ids, gate_vals, gate_up)
        outs, comb = adam_rows(zero, (total,), state, hidden, weight, None, full, 8)
        return (*outs, give_back(comb, tokens.shape[0]))

    core = lax.rem(lax.axis_index("wide"), 2)
    swap_core = lambda a: lax.ppermute(a, "wide", [(i, i ^ 1) for i in range(wide)])
    swap_chip = lambda a: lax.ppermute(a, "wide", [(i, i ^ 2) for i in range(wide)])
    half = full // 2
    sizes = chunks_of(half)
    starts = [sum(sizes[:k]) for k in range(len(sizes))]
    mine, theirs = core * half, (1 - core) * half
    rows_of = lambda a, at, n: lax.dynamic_slice_in_dim(a, at, n, 0)

    lead = swap_core(rows_of(grads, theirs, sizes[0]))
    sent = [swap_chip(rows_of(grads, mine, sizes[0]) + lead)]
    other = swap_core(grads)
    for at, n in zip(starts[1:], sizes[1:]):
        sent.append(swap_chip(rows_of(grads, mine + at, n) + rows_of(other, mine + at, n)))
    hidden, weight = expert_front(tokens, expert_ids, gate_vals, gate_up)
    outs = None
    combs = ([], [])
    for at, n, got in zip(starts, sizes, sent):
        relay = swap_core(got)
        block = 16 if n % 16 == 0 and at % 16 == 0 else 8
        for side, (origin, part) in enumerate(((mine, got), (theirs, relay))):
            outs, comb = adam_rows(
                (origin + at) // block, (grads, other, part), state, hidden, weight, outs, n, block
            )
            combs[side].append(comb)
    ours, rest = (jnp.concatenate(c, axis=0) for c in combs)
    comb = jnp.where(core == 0, jnp.concatenate([ours, rest]), jnp.concatenate([rest, ours]))
    return (*outs, give_back(comb, tokens.shape[0]))


def solution(mesh):
    in_specs = (
        P("wide", "narrow", None),
        P("narrow", None),
        P("narrow", None),
        P("narrow", None),
        P(None, None, "narrow"),
        P(("wide", "narrow"), None),
        P(("wide", "narrow"), None),
        P(("wide", "narrow"), None),
    )
    out_specs = (
        P("narrow", None),
        P("narrow", None),
        P("narrow", None),
        P(("wide", "narrow"), None),
    )
    return jax.shard_map(body, mesh=mesh, in_specs=in_specs, out_specs=out_specs, check_vma=False)
```

```python
import functools

import jax
import jax.numpy as jnp
from jax import lax
from jax.experimental import pallas as pl
from jax.experimental.pallas import tpu as pltpu
from jax.sharding import PartitionSpec as P


EXPERTS = 8
QBLOCK = 128
LANES = 128
VMEM_GRANT = 58 << 20

beta_first = 0.9
beta_second = 0.95
learn_rate = 0.003
adam_eps = 1e-08
quant_limit = 448.0
amax_eps = 1e-06
bias_first = 1.0 - 0.9**10
bias_second = 1.0 - 0.95**10


def adam_kernel(far, block, down, aliased, base, *refs):
    refs = list(refs)
    terms = [refs.pop(0) for _ in range(far[0] + far[1])]
    state = [refs.pop(0) for _ in range(3)]
    if down:
        hidden, weight = refs.pop(0), refs.pop(0)
    refs = refs[4 if aliased else 0 :]
    fresh = [refs.pop(0) for _ in range(3)]
    comb = refs.pop(0) if down else None
    token = refs.pop(0)
    term_v = [refs.pop(0) for _ in terms]
    state_v = [refs.pop(0) for _ in range(3)]
    in_sem, out_sem = refs
    rows, cols = state_v[0].shape
    toks = comb.shape[1] if down else 0

    def copies(j):
        there = pl.ds(pl.multiple_of(base[0] + j * block, 8), block)
        here = pl.ds(pl.multiple_of(j * block, 8), block)
        pairs = [(t.at[there if q < far[0] else here], v) for q, (t, v) in enumerate(zip(terms, term_v))]
        pairs += [(s.at[there], v) for s, v in zip(state, state_v)]
        ins = [
            pltpu.make_async_copy(s, v.at[here], in_sem.at[q, j]) for q, (s, v) in enumerate(pairs)
        ]
        outs = [
            pltpu.make_async_copy(v.at[here], f.at[there], out_sem.at[q, j])
            for q, (v, f) in enumerate(zip(state_v, fresh))
        ]
        return ins, outs, here

    def begin(j, carry):
        for copy in copies(j)[0]:
            copy.start()
        return carry

    def adam(here, at):
        read = lambda ref: ref[here, at].astype(jnp.float32)
        grad = read(term_v[0])
        if far[0] == 2:
            grad = (grad + read(term_v[1])).astype(jnp.bfloat16).astype(jnp.float32)
        if len(term_v) > 1:
            grad = grad + read(term_v[-1])
        first = beta_first * read(state_v[1]) + (1.0 - beta_first) * grad
        second = beta_second * read(state_v[2]) + (1.0 - beta_second) * grad * grad
        state_v[1][here, at] = first
        state_v[2][here, at] = second
        spread = second * (1.0 / bias_second)
        step = first * (learn_rate / bias_first) / (spread * lax.rsqrt(spread) + adam_eps)
        updated = read(state_v[0]) - step
        state_v[0][here, at] = updated.astype(jnp.bfloat16)
        return updated

    def step_down(here):
        slices = weight.shape[0]
        unit = cols // slices
        lanes = hidden.shape[1]
        group = lanes // toks
        lane_block = lax.broadcasted_iota(jnp.int32, (block, lanes), 1) // toks
        total = jnp.zeros((block, lanes), jnp.float32)
        for s in range(slices):
            updated = adam(here, slice(s * unit, (s + 1) * unit))
            partial = jnp.zeros((block, lanes), jnp.float32)
            for g in range(0, unit // QBLOCK, group):
                scales = jnp.zeros((block, lanes), jnp.float32)
                pieces = []
                for b in range(group):
                    cells = updated[:, (g + b) * QBLOCK : (g + b + 1) * QBLOCK]
                    amax = jnp.max(jnp.abs(cells), axis=1, keepdims=True)
                    scale = (amax + amax_eps) * (1.0 / quant_limit)
                    scale = scale.astype(jnp.bfloat16).astype(jnp.float32)
                    scales = jnp.where(lane_block == b, scale, scales)
                    pieces.append((cells * (1.0 / scale)).astype(jnp.bfloat16))
                at = slice(s * unit + g * QBLOCK, s * unit + (g + group) * QBLOCK)
                dots = jnp.dot(
                    jnp.concatenate(pieces, axis=1) if group > 1 else pieces[0],
                    hidden[at, :],
                    preferred_element_type=jnp.float32,
                )
                partial = partial + dots * scales
            turn = toks
            while turn < lanes:
                partial = partial + pltpu.roll(partial, turn, 1)
                turn *= 2
            total = total + partial.astype(jnp.bfloat16).astype(jnp.float32) * weight[s : s + 1, :]
        comb[here, :] = total[:, :toks]

    def step_plain(here):
        width = 1024 if cols % 1024 == 0 else LANES

        def part(c, carry):
            adam(here, pl.ds(pl.multiple_of(c * width, LANES), width))
            return carry

        lax.fori_loop(0, cols // width, part, 0)

    def step(j, carry):
        ins, outs, here = copies(j)
        for copy in ins:
            copy.wait()
        (step_down if down else step_plain)(here)
        for copy in outs:
            copy.start()
        return carry

    def finish(j, carry):
        for copy in copies(j)[1]:
            copy.wait()
        return carry

    token[...] = jnp.zeros_like(token)
    for phase in (begin, step, finish):
        lax.fori_loop(0, rows // block, phase, 0)


def adam_rows(base, whole, local, state, outs, token, rows, block, hidden=None, weight=None, toks=0):
    full, cols = state[0].shape
    down = hidden is not None
    anywhere, vmem = pl.BlockSpec(memory_space=pltpu.HBM), pl.BlockSpec(memory_space=pltpu.VMEM)
    args = [*whole, *local, *state]
    in_specs = [anywhere] * len(whole) + [pl.BlockSpec(memory_space=pl.ANY)] * len(local)
    in_specs += [anywhere] * len(state)
    if down:
        args += [hidden, weight]
        in_specs += [vmem] * 2
    aliases = {}
    if outs is not None:
        aliases = {1 + len(args) + i: i for i in range(3)}
        in_specs += [anywhere] * 3 + [vmem]
        args += [*outs, token]
    terms = len(whole) + len(local)
    cells = rows * cols
    scratch = [pltpu.VMEM((rows, cols), jnp.bfloat16)] * (terms + 1)
    scratch += [pltpu.VMEM((rows, cols), jnp.float32)] * 2
    scratch += [
        pltpu.SemaphoreType.DMA((terms + 3, rows // block)),
        pltpu.SemaphoreType.DMA((3, rows // block)),
    ]
    result = pl.pallas_call(
        functools.partial(adam_kernel, (len(whole), len(local)), block, down, outs is not None),
        grid_spec=pltpu.PrefetchScalarGridSpec(
            num_scalar_prefetch=1,
            grid=(),
            in_specs=in_specs,
            out_specs=[anywhere] * 3 + [vmem] * (1 + down),
            scratch_shapes=scratch,
        ),
        out_shape=[
            jax.ShapeDtypeStruct((full, cols), jnp.bfloat16),
            jax.ShapeDtypeStruct((full, cols), jnp.float32),
            jax.ShapeDtypeStruct((full, cols), jnp.float32),
        ]
        + [jax.ShapeDtypeStruct((rows, toks), jnp.float32)] * down
        + [jax.ShapeDtypeStruct((8, LANES), jnp.float32)],
        input_output_aliases=aliases,
        compiler_params=pltpu.CompilerParams(vmem_limit_bytes=VMEM_GRANT),
        cost_estimate=pl.CostEstimate(
            flops=cells * (40 + 2 * toks),
            bytes_accessed=cells * (20 + 2 * terms),
            transcendentals=cells * 3,
        ),
    )(base.reshape(1), *args)
    return result[:3], result[-1], result[3]


def block_diagonal(hidden, toks):
    cells = hidden.shape[0]
    group = max(1, LANES // toks)
    which = (jnp.arange(cells) // QBLOCK % group)[:, None, None] == jnp.arange(group)[None, :, None]
    out = jnp.where(which, hidden[:, None, :], jnp.zeros((), hidden.dtype))
    return out.reshape(cells, group * toks), group


def token_weights(expert_ids, gate_vals):
    onehot = (expert_ids[:, :, None] == jnp.arange(EXPERTS, dtype=jnp.int32)).astype(jnp.float32)
    return jnp.sum(onehot * gate_vals.astype(jnp.float32)[:, :, None], axis=1).astype(jnp.bfloat16)


def up_project(rows, gate_up):
    proj = jnp.einsum("td,dgu->gtu", rows, gate_up, preferred_element_type=jnp.float32)
    return (jax.nn.silu(proj[0]) * proj[1]).astype(jnp.bfloat16)


def plain_body(grads, state, gate_up, tokens, expert_ids, gate_vals):
    narrow = lax.axis_size("narrow")
    tok_count, width = tokens.shape
    full = grads.shape[0]
    spread = lambda x: lax.all_to_all(
        jnp.broadcast_to(x[None], (narrow,) + x.shape), "narrow", 0, 0, tiled=True
    )
    total = lax.psum(grads, "wide")
    local = jnp.pad(token_weights(expert_ids, gate_vals), ((0, 0), (0, LANES - EXPERTS)))
    toks = narrow * tok_count
    every = spread(jnp.concatenate([tokens, local], axis=1)).reshape(toks, -1)
    hidden = spread(up_project(every[:, :width], gate_up))
    hidden = hidden.transpose(0, 2, 1).reshape(-1, toks)
    hidden, group = block_diagonal(hidden, toks)
    weight = jnp.repeat(every[:, width : width + EXPERTS].T, narrow // EXPERTS, axis=0)
    weight = jnp.tile(weight.astype(jnp.float32), (1, group))
    zero = jnp.zeros((), jnp.int32)
    outs, _, comb = adam_rows(zero, (total,), (), state, None, None, full, 8, hidden, weight, toks)
    out = comb.T.astype(jnp.bfloat16).reshape(narrow, tok_count, full)
    out = lax.all_to_all(out, "narrow", 0, 0, tiled=True)
    return (*outs, out.transpose(1, 0, 2).reshape(tok_count, narrow * full))


together = lax.optimization_barrier


def xor_gather(x, axes, size, groups, early=None, meet=None):
    index = lax.axis_index(axes)
    for turn, bits in enumerate(groups):
        if turn and meet is not None:
            x = meet(x)
        masks = [0]
        for bit in bits:
            masks += [m | bit for m in masks]
        got = [lax.ppermute(x, axes, [(i, i ^ m) for i in range(size)]) for m in masks[1:]]
        got = [x] + got
        if not turn and early is not None:
            got = early(got)
        x = jnp.stack(got).reshape((2,) * len(bits) + x.shape)
        for place, bit in enumerate(bits):
            axis = len(bits) - 1 - place
            x = jnp.where(index & bit, jnp.flip(x, axis), x)
    return x


def row_chunks(half):
    sizes, left = [], half
    for share in CHUNKS:
        take = min(left, max(8, half * share // sum(CHUNKS) // 16 * 16))
        sizes.append(take)
        left -= take
    sizes[0] += left
    return [n for n in sizes if n]


CHUNKS = (80, 48, 48, 32, 16)


def body(grad_parts, master, moment_one, moment_two, gate_up, tokens, expert_ids, gate_vals):
    grads = grad_parts[0]
    full, _ = grads.shape
    wide, narrow = lax.axis_size("wide"), lax.axis_size("narrow")
    state = (master, moment_one, moment_two)
    tok_count, width = tokens.shape
    if wide != 4 or narrow != 8 or full % 32:
        return plain_body(grads, state, gate_up, tokens, expert_ids, gate_vals)

    both = ("wide", "narrow")
    core = lax.axis_index("wide") & 1
    swap_core = lambda a: lax.ppermute(a, "wide", [(i, i ^ 1) for i in range(wide)])
    swap_chip = lambda a: lax.ppermute(a, "wide", [(i, i ^ 2) for i in range(wide)])
    half = full // 2
    sizes = row_chunks(half)
    starts = [sum(sizes[:k]) for k in range(len(sizes))]
    mine, theirs = core * half, (1 - core) * half
    rows_of = lambda a, at, n: lax.dynamic_slice_in_dim(a, at, n, 0)

    lead = swap_core(rows_of(grads, theirs, sizes[0]))
    held, lead = together((grads, lead))
    other = swap_core(held)
    sums = [rows_of(grads, mine, sizes[0]) + lead]
    sums += [
        rows_of(grads, mine + at, n) + rows_of(other, mine + at, n)
        for at, n in zip(starts[1:], sizes[1:])
    ]
    got = []

    def send(k):
        got.append(swap_chip(sums[k]))

    def send_first(x):
        x, sums[0] = together((x, sums[0]))
        send(0)
        return x

    def send_rest(x):
        x, *sums[1:] = together((x, *sums[1:]))
        for k in range(1, len(sums)):
            send(k)
        return x

    toks = 2 * narrow * tok_count
    every = xor_gather(tokens, both, wide * narrow, ((1, narrow), (2, 4)), send_first)
    every = every.transpose(2, 0, 1, 3, 4, 5).reshape(toks, width)
    piece = up_project(every, gate_up)
    local = jnp.pad(token_weights(expert_ids, gate_vals), ((0, 0), (0, LANES - EXPERTS)))
    local = xor_gather(local, "wide", wide, ((1,),)).reshape(2 * tok_count, LANES)
    local = jnp.pad(local, ((0, toks - 2 * tok_count), (0, 0)))
    piece = jnp.concatenate([piece, local], axis=1)
    hidden = xor_gather(piece, "narrow", narrow, ((1,), (2, 4)), None, send_rest)
    hidden = hidden.reshape(narrow, toks, -1)
    unit = gate_up.shape[2]
    weight = hidden[:, : 2 * tok_count, unit : unit + EXPERTS]
    weight = weight.reshape(narrow, 2, tok_count, EXPERTS).transpose(3, 1, 0, 2).reshape(EXPERTS, toks)
    hidden = hidden[:, :, :unit].transpose(0, 2, 1).reshape(-1, toks)
    hidden, group = block_diagonal(hidden, toks)
    weight = jnp.tile(jnp.repeat(weight.astype(jnp.float32), narrow // EXPERTS, axis=0), (1, group))

    outs, combs, token = None, [], None
    for k, (at, n) in enumerate(zip(starts, sizes)):
        if k:
            got[k], token = together((got[k], token))
        relay = swap_core(got[k])
        own = lambda outs, token: adam_rows(
            mine + at, (), (sums[k], got[k]), state, outs, token, n, 16, hidden, weight, toks
        )
        rest = lambda outs, token: adam_rows(theirs + at, (grads, other), (relay,), state, outs, token, n, 16)
        if k == 0:
            outs, token, _ = rest(outs, token)
        outs, token, comb = own(outs, token)
        combs.append(comb)
        if k:
            outs, token, _ = rest(outs, token)
    out = jnp.concatenate(combs, axis=0).T.astype(jnp.bfloat16).reshape(2 * narrow, tok_count, half)
    groups = [[(2 * x + c) * narrow + n for c in range(2) for n in range(narrow)] for x in range(wide // 2)]
    out = lax.all_to_all(out, both, 0, 0, axis_index_groups=groups, tiled=True)
    out = out.reshape(2, narrow, tok_count, half).transpose(2, 1, 0, 3).reshape(tok_count, narrow * full)
    return (*outs, out)


def solution(mesh):
    in_specs = (
        P("wide", "narrow", None),
        P("narrow", None),
        P("narrow", None),
        P("narrow", None),
        P(None, None, "narrow"),
        P(("wide", "narrow"), None),
        P(("wide", "narrow"), None),
        P(("wide", "narrow"), None),
    )
    out_specs = (
        P("narrow", None),
        P("narrow", None),
        P("narrow", None),
        P(("wide", "narrow"), None),
    )
    return jax.shard_map(body, mesh=mesh, in_specs=in_specs, out_specs=out_specs, check_vma=False)
```

```python
import functools

import jax
import jax.numpy as jnp
from jax import lax
from jax.experimental import pallas as pl
from jax.experimental.pallas import tpu as pltpu
from jax.sharding import PartitionSpec as P


EXPERTS = 8
QBLOCK = 128
LANES = 128
VMEM_GRANT = 40 << 20

beta_first = 0.9
beta_second = 0.95
learn_rate = 0.003
adam_eps = 1e-08
quant_limit = 448.0
amax_eps = 1e-06
bias_first = 1.0 - 0.9**10
bias_second = 1.0 - 0.95**10


def adam_kernel(shared, runs, block, down, aliased, base, *refs):
    refs = list(refs)
    whole = [refs.pop(0) for _ in range(shared)]
    local = [[refs.pop(0) for _ in range(own)] for _, own, _ in runs]
    state = [refs.pop(0) for _ in range(3)]
    counts = [rows for rows, _, _ in runs]
    if down:
        hidden, weight = [refs.pop(0) for _ in range(down)], refs.pop(0)
    refs = refs[4 if aliased else 0 :]
    fresh = [refs.pop(0) for _ in range(3)]
    comb = refs.pop(0) if down else None
    token = refs.pop(0)
    term_v = [refs.pop(0) for _ in range(3)]
    state_v = [refs.pop(0) for _ in range(3)]
    acc = refs.pop(0) if down else None
    in_sem, out_sem = refs
    cols = state_v[0].shape[1]
    toks = comb.shape[0] if down else 0

    def copies(run, j):
        slot = sum(counts[:run]) // block + j
        there = pl.ds(pl.multiple_of(base[run] + j * block, 8), block)
        here = pl.ds(pl.multiple_of(slot * block, 8), block)
        near = pl.ds(pl.multiple_of(j * block, 8), block)
        far = () if runs[run][2] and local[run] else whole
        pairs = [(a.at[there], v) for a, v in zip(far, term_v)]
        pairs += [(a.at[near], v) for a, v in zip(local[run], term_v[len(far) :])]
        pairs += [(a.at[there], v) for a, v in zip(state, state_v)]
        ins = [
            pltpu.make_async_copy(a, v.at[here], in_sem.at[q, slot]) for q, (a, v) in enumerate(pairs)
        ]
        outs = [
            pltpu.make_async_copy(v.at[here], f.at[there], out_sem.at[q, slot])
            for q, (v, f) in enumerate(zip(state_v, fresh))
        ]
        return ins, outs, here

    def begin(run, j, carry):
        for copy in copies(run, j)[0]:
            copy.start()
        return carry

    def adam(terms, here, at):
        read = lambda ref: ref[here, at].astype(jnp.float32)
        grad = read(term_v[0])
        if terms == 3:
            grad = (grad + read(term_v[1])).astype(jnp.bfloat16).astype(jnp.float32)
        if terms > 1:
            grad = grad + read(term_v[terms - 1])
        first = beta_first * read(state_v[1]) + (1.0 - beta_first) * grad
        second = beta_second * read(state_v[2]) + (1.0 - beta_second) * grad * grad
        state_v[1][here, at] = first
        state_v[2][here, at] = second
        spread = second * (1.0 / bias_second)
        step = first * (learn_rate / bias_first) / (spread * lax.rsqrt(spread) + adam_eps)
        updated = read(state_v[0]) - step
        state_v[0][here, at] = updated.astype(jnp.bfloat16)
        return updated

    def step_down(terms, here):
        slices = weight.shape[0]
        unit = cols // slices
        total = jnp.zeros((block, toks), jnp.float32)
        for s in range(slices):
            updated = adam(terms, here, slice(s * unit, (s + 1) * unit))
            partial = jnp.zeros((block, toks), jnp.float32)
            for b in range(unit // QBLOCK):
                cut = slice(b * QBLOCK, (b + 1) * QBLOCK)
                cells = updated[:, cut]
                amax = jnp.max(jnp.abs(cells), axis=1, keepdims=True)
                scale = (amax + amax_eps) * (1.0 / quant_limit)
                scale = scale.astype(jnp.bfloat16).astype(jnp.float32)
                quanta = (cells * (1.0 / scale)).astype(jnp.bfloat16)
                dots = lax.dot_general(
                    quanta,
                    jnp.concatenate([h[s, :, cut] for h in hidden], axis=0),
                    (((1,), (1,)), ((), ())),
                    preferred_element_type=jnp.float32,
                )
                partial = partial + scale * dots
            total = total + partial.astype(jnp.bfloat16).astype(jnp.float32) * weight[s : s + 1, :]
        acc[here, :] = total

    def step_plain(terms, here):
        width = 1024 if cols % 1024 == 0 else LANES

        def part(c, carry):
            adam(terms, here, pl.ds(pl.multiple_of(c * width, LANES), width))
            return carry

        lax.fori_loop(0, cols // width, part, 0)

    def step(run, j, carry):
        ins, outs, here = copies(run, j)
        for copy in ins:
            copy.wait()
        _, own, products = runs[run]
        terms = own + (0 if products and own else shared)
        (step_down if products else step_plain)(terms, here)
        for copy in outs:
            copy.start()
        return carry

    def finish(run, j, carry):
        for copy in copies(run, j)[1]:
            copy.wait()
        return carry

    token[...] = jnp.zeros_like(token)
    for phase in (begin, step, finish):
        for run, rows in enumerate(counts):
            lax.fori_loop(0, rows // block, functools.partial(phase, run), 0)
        if phase is step and down:
            ones = (
                lax.broadcasted_iota(jnp.int32, (toks, toks), 0)
                == lax.broadcasted_iota(jnp.int32, (toks, toks), 1)
            ).astype(jnp.bfloat16)
            comb[...] = lax.dot_general(
                ones,
                acc[: comb.shape[1], :].astype(jnp.bfloat16),
                (((1,), (1,)), ((), ())),
                preferred_element_type=jnp.float32,
            ).astype(jnp.bfloat16)


def adam_rows(runs, whole, state, outs, token, block, hidden=(), weight=None):
    full, cols = state[0].shape
    counts = [count for _, count, _, _ in runs]
    rows = sum(counts)
    made = sum(count for _, count, _, products in runs if products)
    down = len(hidden)
    toks = sum(h.shape[1] for h in hidden)
    hbm, vmem = pl.BlockSpec(memory_space=pltpu.HBM), pl.BlockSpec(memory_space=pltpu.VMEM)
    parts = [a for _, _, own, _ in runs for a in own]
    far = lambda a: pltpu.with_memory_space_constraint(a, pltpu.HBM)
    args = [*map(far, whole), *parts, *map(far, state)]
    in_specs = [hbm] * len(whole) + [pl.BlockSpec(memory_space=pl.ANY)] * len(parts)
    in_specs += [hbm] * len(state)
    if down:
        args += [*hidden, weight]
        in_specs += [vmem] * (down + 1)
    aliases = {}
    if outs is not None:
        aliases = {1 + len(args) + i: i for i in range(3)}
        in_specs += [hbm] * 3 + [vmem]
        args += [*outs, token]
    cells = rows * cols
    scratch = [pltpu.VMEM((rows, cols), jnp.bfloat16)] * 4
    scratch += [pltpu.VMEM((rows, cols), jnp.float32)] * 2
    if down:
        scratch.append(pltpu.VMEM((rows, toks), jnp.float32))
    scratch += [
        pltpu.SemaphoreType.DMA((6, rows // block)),
        pltpu.SemaphoreType.DMA((3, rows // block)),
    ]
    result = pl.pallas_call(
        functools.partial(
            adam_kernel,
            len(whole),
            tuple((count, len(own), products) for _, count, own, products in runs),
            block,
            down,
            outs is not None,
        ),
        grid_spec=pltpu.PrefetchScalarGridSpec(
            num_scalar_prefetch=1,
            grid=(),
            in_specs=in_specs,
            out_specs=[hbm] * 3 + [vmem] * (1 + bool(down)),
            scratch_shapes=scratch,
        ),
        out_shape=[
            jax.ShapeDtypeStruct((full, cols), jnp.bfloat16),
            jax.ShapeDtypeStruct((full, cols), jnp.float32),
            jax.ShapeDtypeStruct((full, cols), jnp.float32),
        ]
        + [jax.ShapeDtypeStruct((toks, made), jnp.bfloat16)] * bool(down)
        + [jax.ShapeDtypeStruct((8, LANES), jnp.float32)],
        input_output_aliases=aliases,
        compiler_params=pltpu.CompilerParams(vmem_limit_bytes=VMEM_GRANT),
        cost_estimate=pl.CostEstimate(
            flops=cells * (40 + 2 * toks),
            bytes_accessed=cells * 26,
            transcendentals=cells * 3,
        ),
    )(jnp.stack([run[0] for run in runs]).astype(jnp.int32), *args)
    return result[:3], result[-1], result[3]


def token_weights(expert_ids, gate_vals):
    onehot = (expert_ids[:, :, None] == jnp.arange(EXPERTS, dtype=jnp.int32)).astype(jnp.float32)
    return jnp.sum(onehot * gate_vals.astype(jnp.float32)[:, :, None], axis=1).astype(jnp.bfloat16)


def up_project(rows, gate_up):
    proj = jnp.einsum("td,dgu->gtu", rows, gate_up, preferred_element_type=jnp.float32)
    return (jax.nn.silu(proj[0]) * proj[1]).astype(jnp.bfloat16)


def plain_body(grads, state, gate_up, tokens, expert_ids, gate_vals):
    narrow = lax.axis_size("narrow")
    tok_count, width = tokens.shape
    full = grads.shape[0]
    spread = lambda x: lax.all_to_all(
        jnp.broadcast_to(x[None], (narrow,) + x.shape), "narrow", 0, 0, tiled=True
    )
    total = lax.psum(grads, "wide")
    local = jnp.pad(token_weights(expert_ids, gate_vals), ((0, 0), (0, LANES - EXPERTS)))
    toks = narrow * tok_count
    every = spread(jnp.concatenate([tokens, local], axis=1)).reshape(toks, -1)
    hidden = spread(up_project(every[:, :width], gate_up))
    weight = jnp.repeat(every[:, width : width + EXPERTS].T, narrow // EXPERTS, axis=0)
    weight = weight.astype(jnp.float32)
    zero = jnp.zeros((), jnp.int32)
    runs = [(zero, full, (), True)]
    outs, _, comb = adam_rows(runs, (total,), state, None, None, 8, (hidden,), weight)
    out = comb.reshape(narrow, tok_count, full)
    out = lax.all_to_all(out, "narrow", 0, 0, tiled=True)
    return (*outs, out.transpose(1, 0, 2).reshape(tok_count, narrow * full))


together = lax.optimization_barrier


def row_chunks(half):
    sizes, left = [], half
    for share in CHUNKS:
        take = min(left, max(8, half * share // sum(CHUNKS) // 16 * 16))
        sizes.append(take)
        left -= take
    sizes[0] += left
    return [n for n in sizes if n]


CHUNKS = (48, 64, 48, 32, 32)


def body(grad_parts, master, moment_one, moment_two, gate_up, tokens, expert_ids, gate_vals):
    grads = grad_parts[0]
    full, cols = grads.shape
    wide, narrow = lax.axis_size("wide"), lax.axis_size("narrow")
    state = (master, moment_one, moment_two)
    tok_count, width = tokens.shape
    if wide != 4 or narrow != 8 or full % 32:
        return plain_body(grads, state, gate_up, tokens, expert_ids, gate_vals)

    both = ("wide", "narrow")
    core = lax.axis_index("wide") & 1
    swap_core = lambda a: lax.ppermute(a, "wide", [(i, i ^ 1) for i in range(wide)])
    swap_chip = lambda a: lax.ppermute(a, "wide", [(i, i ^ 2) for i in range(wide)])
    half = full // 2
    sizes = row_chunks(half)
    starts = [sum(sizes[:k]) for k in range(len(sizes))]
    mine, theirs = core * half, (1 - core) * half

    def rows_of(a, at, n):
        tiles = lax.dynamic_slice_in_dim(a.reshape(full // 16, 16, cols), at // 16, n // 16, 0)
        return tiles.reshape(n, cols)

    lead = swap_core(rows_of(grads, theirs, sizes[0]))
    held, lead = together((grads, lead))
    other = swap_core(held)
    sums = [rows_of(grads, mine, sizes[0]) + lead]

    def send(k):
        return swap_chip(sums[k])

    got = [send(0)]
    other, sums[0] = together((other, sums[0]))
    sum_of = lambda k: rows_of(grads, mine + starts[k], sizes[k]) + rows_of(other, mine + starts[k], sizes[k])
    sums.append(sum_of(1))

    def spread(x):
        x = jnp.broadcast_to(x[None], (narrow, *x.shape))
        return lax.all_to_all(x, "narrow", 0, 0, tiled=True)

    toks = narrow * tok_count
    local = jnp.pad(token_weights(expert_ids, gate_vals), ((0, 0), (0, LANES - EXPERTS)))
    packed = jnp.concatenate([tokens, local], axis=1)
    every = spread(packed)
    every, sums[1] = together((every, sums[1]))
    got.append(send(1))
    every = every.reshape(toks, -1)
    chosen = every[:, width : width + EXPERTS]
    theirs_chosen = swap_core(chosen)
    weight = jnp.concatenate([chosen, theirs_chosen]).T.astype(jnp.float32)
    weight = jnp.repeat(weight, narrow // EXPERTS, axis=0)
    piece = up_project(every[:, :width], gate_up)
    piece, other = together((piece, other))
    hidden = spread(piece)
    for k in range(2, len(sizes)):
        sums.append(sum_of(k))
        got.append(send(k))
    hidden = (hidden, swap_core(hidden))

    outs, combs, token, relays = None, [], None, []

    def relay(k):
        nonlocal token
        if token is not None:
            got[k], token = together((got[k], token))
        relays.append(swap_core(got[k]))

    def update(own=(), rest=()):
        nonlocal outs, token
        runs = [(mine + starts[k], sizes[k], (sums[k], got[k]), True) for k in own]
        runs += [(theirs + starts[k], sizes[k], (relays[k],), False) for k in rest]
        whole = (grads, other) if rest else ()
        extra = (hidden, weight) if own else ()
        outs, token, comb = adam_rows(runs, whole, state, outs, token, 16, *extra)
        if own:
            combs.append(comb)

    relay(0)
    relays[0], weight = together((relays[0], weight))
    update(rest=(0,))
    relay(1)
    update(own=(0, 1), rest=(1,))
    relay(2)
    update(own=(2,), rest=(2,))
    for k in range(3, len(sizes)):
        relay(k)
        update(own=(k,))
        update(rest=(k,))
    out = jnp.concatenate(combs, axis=1).reshape(2, narrow, tok_count, half)
    out = jnp.where(core == 0, out, out[::-1]).reshape(2 * narrow, tok_count, half)
    groups = [[(2 * x + c) * narrow + n for c in range(2) for n in range(narrow)] for x in range(wide // 2)]
    out = lax.all_to_all(out, both, 0, 0, axis_index_groups=groups, tiled=True)
    out = out.reshape(2, narrow, tok_count, half).transpose(2, 1, 0, 3).reshape(tok_count, narrow * full)
    return (*outs, out)


def solution(mesh):
    in_specs = (
        P("wide", "narrow", None),
        P("narrow", None),
        P("narrow", None),
        P("narrow", None),
        P(None, None, "narrow"),
        P(("wide", "narrow"), None),
        P(("wide", "narrow"), None),
        P(("wide", "narrow"), None),
    )
    out_specs = (
        P("narrow", None),
        P("narrow", None),
        P("narrow", None),
        P(("wide", "narrow"), None),
    )
    return jax.shard_map(body, mesh=mesh, in_specs=in_specs, out_specs=out_specs, check_vma=False)
```
